32 devices in a mesh: swath: 8 (over y, x, core), chan: 4 (over z).
Axes of the slice: x: 2, y: 2, z: 4, core: 2. Of those that a mesh axis runs over, the one named last changes fastest.
Arguments:
- innovations: float32 [524288], P(('swath', 'chan')), may hold values from -6 to 6
- obs_precision: float32 [524288], P(('swath', 'chan')), may hold values from 0.25 to 4
- jacobian: bfloat16 [524288, 128], P(('swath', 'chan')), may hold values from -0.5 to 0.5
- predictors: float32 [8, 524288], P(None, ('swath', 'chan')), may hold values from -5 to 5
- obs_column: int32 [524288], P(('swath', 'chan')), may hold values from 0 to 2047, as said below
- obs_channel: int32 [524288], P(('swath', 'chan')), may hold values from 0 to 5119
- obs_count: int32 [8, 4], P('swath', 'chan'), may hold values from 5461 to 16384, as said below
- smoothing: float32 [128], replicated, may hold values from 0.02 to 0.12
- bias_precision: float32 [8, 5120], P(None, 'chan'), may hold values from 1 to 100
Outputs:
- control_state: float32 [256, 256, 128], P('swath', 'chan')
- bias_increment: float32 [8, 5120], P(None, 'chan')
- residual_norms: float32 [3], replicated
The draws below stay inside these ranges and needn't reach their ends.
Inputs may be any that keep to these rules, and one draw needn't show every extreme that they name: `obs_column`: Row-major index latitude row * 64 + longitude column within the tile of the device that holds the slot; all slots of an aligned block of 128 slots lie in one latitude row. `obs_channel`: channel c belongs to block c // 256, whose coefficients are owned by chan index c // 1280. `obs_count`: slots below the count hold live observations, the rest are ignored; some device is full in every draw.
All inputs are finite; a program needn't handle non-finite values.
Results may differ from the reference program's by a relative error of at most 0.0003.
Values sent between devices are 32-bit elements; how exact they have to be, the bound alone decides.
A program may use at most 128 MiB of HBM per device.

```python
import math
import jax
import jax.numpy as jnp
from jax import lax

LEV = 128
NPRED = 8
OBS_BLOCK = 128
LAT_DEV = 32
LON_DEV = 64
OBS_DEV = 16384
ITERS = 2
OBS_ALL = 524288
CHANNELS = 5120
N_SWATH = 8
N_CHAN = 4


def draw_obs_count(key, part):
    devices_all = N_SWATH * N_CHAN
    counts = jax.random.randint(jax.random.fold_in(key, 11), (devices_all,), OBS_DEV // 3, OBS_DEV + 1)
    fullest = jax.random.randint(jax.random.fold_in(key, 12), (), 0, devices_all)
    counts = jnp.where(jnp.arange(devices_all) == fullest, OBS_DEV, counts)
    return counts.reshape(N_SWATH, N_CHAN).astype(jnp.int32)


def draw_obs_column(key, part):
    block_count = OBS_DEV * N_SWATH * N_CHAN // OBS_BLOCK
    line_rows = jax.random.randint(jax.random.fold_in(key, 21), (block_count,), 0, LAT_DEV)
    line_cols = jax.random.randint(jax.random.fold_in(key, 22), (block_count, OBS_BLOCK), 0, LON_DEV)
    return (line_rows[:, None] * LON_DEV + line_cols).reshape(-1).astype(jnp.int32)


def touch_ends(entries, rng, smallest, largest):
    longest = entries.shape.index(max(entries.shape))
    spots = []
    for shift in (0, 1):
        where = [jax.random.randint(jax.random.fold_in(rng, axis), (), 0, length) for axis, length in enumerate(entries.shape)]
        where[longest] = (where[longest] + shift) % entries.shape[longest]
        spots.append(tuple(where))
    return entries.at[spots[0]].set(smallest).at[spots[1]].set(largest)


def steps_of(own_key, dims, split, least, top_value):
    def one(axis_at, blocks):
        draws = jax.random.uniform(jax.random.fold_in(jax.random.fold_in(own_key, 6), axis_at), (blocks,), jnp.float32, least / len(split), top_value / len(split))
        return jnp.repeat(jnp.exp(draws), dims[axis_at] // blocks).reshape((-1,) + (1,) * (len(dims) - axis_at - 1))

    level = one(*split[0])
    for cut in split[1:]:
        level = level * one(*cut)
    return level


def centred(own_key, shape, deviation, most, pieces=(), kind=jnp.bfloat16):
    result = jax.random.normal(own_key, shape, jnp.float32) * deviation
    if len(pieces) > 0:
        result = steps_of(own_key, shape, pieces, -0.22, 0.18) * result
    return jnp.clip(result, min=-most, max=most).astype(kind)


def setup_inputs(seed: int = 0) -> dict:
    arg_keys = jax.random.split(jax.random.key(seed), 10)
    innovations = centred(arg_keys[0], (OBS_ALL,), 1.0, 6.0, ((0, 32),), jnp.float32)
    obs_precision = jnp.clip(jnp.exp(math.log(4.0) - 2.7725887 * jax.random.uniform(arg_keys[1], (OBS_ALL,), jnp.float32) ** steps_of(arg_keys[1], (OBS_ALL,), ((0, 32),), -0.2, 0.2)), 0.25, 4.0)
    jacobian = centred(arg_keys[2], (OBS_ALL, LEV), LEV ** -0.5, 0.5, ((0, 32),))
    predictors = centred(arg_keys[3], (NPRED, OBS_ALL), 1.0, 5.0, ((1, 32),), jnp.float32)
    obs_column = draw_obs_column(jax.random.fold_in(arg_keys[9], 71), 0)
    obs_channel = touch_ends(jax.random.randint(arg_keys[5], (OBS_ALL,), 0, CHANNELS), jax.random.fold_in(arg_keys[5], 1), 0, CHANNELS - 1).astype(jnp.int32)
    obs_count = draw_obs_count(jax.random.fold_in(arg_keys[9], 71), 0)
    smoothing = jnp.clip(jnp.exp(jax.random.uniform(arg_keys[7], (LEV,), jnp.float32, math.log(0.02), math.log(0.12))), 0.02, 0.12)
    bias_precision = jnp.clip(jnp.exp(math.log(100.0) - 4.6051702 * jax.random.uniform(arg_keys[8], (NPRED, CHANNELS), jnp.float32) ** steps_of(arg_keys[8], (NPRED, CHANNELS), ((1, 4),), -0.2, 0.2)), 1.0, 100.0)
    return dict(innovations=innovations, obs_precision=obs_precision, jacobian=jacobian, predictors=predictors, obs_column=obs_column, obs_channel=obs_channel, obs_count=obs_count, smoothing=smoothing, bias_precision=bias_precision)


def smooth_field(state_field, smoothing):
    padded = jnp.pad(state_field, ((1, 1), (0, 0), (0, 0)))
    beside = padded[:-2] + padded[2:] + jnp.roll(state_field, 1, axis=1) + jnp.roll(state_field, -1, axis=1)
    return state_field + smoothing * (beside - 4.0 * state_field)

def reference(innovations, obs_precision, jacobian, predictors, obs_column, obs_channel, obs_count, smoothing, bias_precision):
    devices_all = N_SWATH * N_CHAN
    lat_all = LAT_DEV * N_SWATH
    lon_all = LON_DEV * N_CHAN
    cells_all = lat_all * lon_all
    slot_ids = jnp.arange(devices_all * OBS_DEV, dtype=jnp.int32)
    holder = slot_ids // OBS_DEV
    row_index = holder // N_CHAN * LAT_DEV + obs_column // LON_DEV
    col_index = holder % N_CHAN * LON_DEV + obs_column % LON_DEV
    flat_cell = (row_index * lon_all + col_index).astype(jnp.int32)
    live = slot_ids % OBS_DEV < obs_count.reshape(-1)[holder]
    weights = jnp.where(live, obs_precision, jnp.zeros_like(obs_precision))
    jac_blocks = jacobian.reshape(devices_all, OBS_DEV, LEV)
    cell_blocks = flat_cell.reshape(devices_all, OBS_DEV)

    def forward(state_field):
        table = state_field.reshape(cells_all, LEV)

        def one_block(pair):
            return lax.optimization_barrier(jnp.sum(pair[0].astype(jnp.float32) * table[pair[1]], axis=1))
        return lax.map(one_block, (jac_blocks, cell_blocks)).reshape(-1)

    def adjoint(values):
        value_blocks = values.reshape(devices_all, OBS_DEV)

        def add_block(table, triple):
            return (table.at[triple[1]].add(triple[0].astype(jnp.float32) * triple[2][:, None]), 0)
        start_table = jnp.zeros((cells_all, LEV), jnp.float32)
        table = lax.scan(add_block, start_table, (jac_blocks, cell_blocks, value_blocks))[0]
        return table.reshape(lat_all, lon_all, LEV)

    def bias_forward(coefs):
        return lax.optimization_barrier(jnp.sum(predictors * coefs[:, obs_channel], axis=0))

    def bias_adjoint(terms):
        return jnp.zeros((NPRED, CHANNELS), jnp.float32).at[:, obs_channel].add(terms)

    def hessian(state_dir, bias_dir):
        image = weights * (forward(smooth_field(state_dir, smoothing)) + bias_forward(bias_dir))
        return (state_dir + smooth_field(adjoint(image), smoothing), bias_precision * bias_dir + bias_adjoint(predictors * image[None, :]))
    source = weights * innovations
    res_state = smooth_field(adjoint(source), smoothing)
    res_bias = bias_adjoint(predictors * source[None, :])
    diagonal = bias_precision + bias_adjoint(predictors * predictors * weights[None, :])
    sol_state = jnp.zeros_like(res_state)
    sol_bias = jnp.zeros_like(res_bias)
    pre_bias = res_bias / diagonal
    dir_state, dir_bias = (res_state, pre_bias)
    state_sq = jnp.sum(res_state * res_state)
    rz_now = state_sq + jnp.sum(res_bias * pre_bias)
    record = [state_sq + jnp.sum(res_bias * res_bias)]
    for turn_index in range(ITERS):
        img_state, img_bias = hessian(dir_state, dir_bias)
        length = rz_now / (jnp.sum(dir_state * img_state) + jnp.sum(dir_bias * img_bias))
        sol_state = sol_state + length * dir_state
        sol_bias = sol_bias + length * dir_bias
        res_state = res_state - length * img_state
        res_bias = res_bias - length * img_bias
        pre_bias = res_bias / diagonal
        state_sq = jnp.sum(res_state * res_state)
        rz_next = state_sq + jnp.sum(res_bias * pre_bias)
        record.append(state_sq + jnp.sum(res_bias * res_bias))
        ratio = rz_next / rz_now
        dir_state = res_state + ratio * dir_state
        dir_bias = pre_bias + ratio * dir_bias
        rz_now = rz_next
    return (sol_state, sol_bias, jnp.sqrt(jnp.stack(record)))
```

```python
import functools

import jax
import jax.numpy as jnp
from jax import lax
from jax.experimental import pallas as pl
from jax.experimental.pallas import tpu as pltpu
from jax.sharding import PartitionSpec as P

LEV = 128
NPRED = 8
CH_BLOCK = 256
OBS_BLOCK = 128
LAT_DEV = 32
LON_DEV = 64
ITERS = 2
LINES = 8
LANES = 128
F32 = jnp.float32
BF16 = jnp.bfloat16
NT = (((1,), (1,)), ((), ()))
VMEM_LIMIT = 60 * 1024 * 1024


def halves(value):
    high = value.astype(BF16)
    return high, (value - high.astype(F32)).astype(BF16)


def local_kernel(init, blocks, rows_ref, count_ref, cell_ref, chan_ref, prec_ref, pred_ref, jac_ref, *refs):
    if init:
        innov_ref, bp_ref, field_ref, cols_ref, table_ref, acc_ref = refs
    else:
        u_ref, coef_ref, field_ref, cols_ref, table_ref, acc_ref, split_ref, flat_ref = refs
    n_lines = cell_ref.shape[0]
    rows_tab = NPRED * blocks
    tables = 2 if init else 1
    count = count_ref[0, 0]
    field_ref[...] = jnp.zeros_like(field_ref)
    acc_ref[...] = jnp.zeros_like(acc_ref)

    if not init:
        def split_row(i, carry):
            high, low = halves(u_ref[i])
            split_ref[i] = jnp.concatenate([high, low], axis=0)
            return carry

        lax.fori_loop(0, LAT_DEV, split_row, 0)
        for b in range(blocks):
            for h in range(CH_BLOCK // LANES):
                block = coef_ref[b * (CH_BLOCK // LANES) + h]
                flat_ref[b * NPRED : (b + 1) * NPRED, h * LANES : (h + 1) * LANES] = block
        high, low = halves(flat_ref[...])
        coef2 = jnp.concatenate([high, low], axis=0)

    iota_col = lax.broadcasted_iota(jnp.int32, (LON_DEV, OBS_BLOCK), 0)
    iota_ch = lax.broadcasted_iota(jnp.int32, (CH_BLOCK, OBS_BLOCK), 0)
    iota_obs = lax.broadcasted_iota(jnp.int32, (1, OBS_BLOCK), 1)

    def step(it, carry):
        base = pl.multiple_of(it * LINES, LINES)
        cells = cell_ref[pl.ds(base, LINES), :]
        chans = chan_ref[pl.ds(base, LINES), :]
        precs = prec_ref[pl.ds(base, LINES), :]
        if init:
            innovs = innov_ref[pl.ds(base, LINES), :]
        hots, his, masks, weights, preds, jacs, rows = [], [], [], [], [], [], []
        for l in range(LINES):
            ch = chans[l : l + 1, :]
            hots.append(jnp.where(iota_ch == ch % CH_BLOCK, 1.0, 0.0).astype(BF16))
            his.append(jnp.broadcast_to(ch // CH_BLOCK, (NPRED, OBS_BLOCK)))
            masks.append(iota_col == cells[l : l + 1, :] % LON_DEV)
            slot = (base + l) * OBS_BLOCK + iota_obs
            weights.append(jnp.where(slot < count, precs[l : l + 1, :], 0.0))
            start = pl.multiple_of((base + l) * OBS_BLOCK, OBS_BLOCK)
            preds.append(pred_ref[:, pl.ds(start, OBS_BLOCK)])
            jacs.append(jac_ref[pl.ds(start, OBS_BLOCK), :])
            rows.append(rows_ref[base + l])
        values = []
        if init:
            for l in range(LINES):
                values.append(weights[l] * innovs[l : l + 1, :])
        else:
            looked = []
            for l in range(0, LINES, 2):
                pair = jnp.concatenate(hots[l : l + 2], axis=1)
                mid = jnp.dot(coef2, pair, preferred_element_type=F32)
                for j in range(2):
                    total = jnp.zeros((NPRED, OBS_BLOCK), F32)
                    lanes = slice(j * OBS_BLOCK, (j + 1) * OBS_BLOCK)
                    for b in range(blocks):
                        top = mid[b * NPRED : (b + 1) * NPRED, lanes]
                        low = mid[rows_tab + b * NPRED : rows_tab + (b + 1) * NPRED, lanes]
                        total = total + jnp.where(his[l + j] == b, top + low, 0.0)
                    looked.append(jnp.sum(total * preds[l + j], axis=0, keepdims=True))
            for l in range(LINES):
                prod = lax.dot_general(split_ref[rows[l]], jacs[l], NT, preferred_element_type=F32)
                both = prod[:LON_DEV] + prod[LON_DEV:]
                seen = jnp.sum(jnp.where(masks[l], both, 0.0), axis=0, keepdims=True)
                values.append(weights[l] * (seen + looked[l]))
        outs = []
        for l in range(LINES):
            high, low = halves(jnp.where(masks[l], values[l], 0.0))
            spread = jnp.concatenate([high, low], axis=0)
            out = jnp.dot(spread, jacs[l], preferred_element_type=F32)
            outs.append(out[:LON_DEV] + out[LON_DEV:])
        for l in range(LINES):
            field_ref[rows[l]] += outs[l]
        lefts = []
        for l in range(LINES):
            pieces = []
            terms = [preds[l] * values[l]]
            if init:
                terms.append(preds[l] * preds[l] * weights[l])
            for term in terms:
                wide = jnp.concatenate(
                    [jnp.where(his[l] == b, term, 0.0) for b in range(blocks)], axis=0
                )
                pieces.extend(halves(wide))
            lefts.append(jnp.concatenate(pieces, axis=0))
        left = jnp.concatenate(lefts, axis=1)
        hot = jnp.concatenate(hots, axis=1)
        acc_ref[...] += lax.dot_general(left, hot, NT, preferred_element_type=F32)
        return carry

    lax.fori_loop(0, n_lines // LINES, step, 0)
    per = CH_BLOCK // LANES
    used = tables * blocks * per
    for t in range(tables):
        for b in range(blocks):
            for h in range(per):
                top = t * 2 * rows_tab + b * NPRED
                low = top + rows_tab
                lanes = slice(h * LANES, (h + 1) * LANES)
                table_ref[(t * blocks + b) * per + h] = (
                    acc_ref[top : top + NPRED, lanes] + acc_ref[low : low + NPRED, lanes]
                )
    if init:
        table_ref[used : used + bp_ref.shape[0]] = bp_ref[...]
        used += bp_ref.shape[0]
    if table_ref.shape[0] > used:
        table_ref[used:] = jnp.zeros((table_ref.shape[0] - used, NPRED, LANES), F32)

    def column(i, carry):
        cols_ref[0, pl.ds(i, 1), :] = field_ref[i, 0:1, :]
        cols_ref[1, pl.ds(i, 1), :] = field_ref[i, LON_DEV - 1 : LON_DEV, :]
        return carry

    lax.fori_loop(0, LAT_DEV, column, 0)


def fold(value):
    total = value[0:8]
    for i in range(1, value.shape[0] // 8):
        total = total + value[8 * i : 8 * i + 8]
    return total


def comm_kernel(n, m, width, mode, *refs):
    refs = list(refs)
    take = lambda k: [refs.pop(0) for _ in range(k)]
    smooth_ref, g_ref, gc_ref, table_ref = take(4)
    if mode == "first":
        r_out, rc_ref, u_out, rb_out, diag_out, bp_out, pb_out, scal_out = take(8)
    else:
        p_ref, r_ref, pb_ref, rb_ref, diag_ref, bp_ref, scal_ref = take(7)
        if mode == "middle":
            u_ref, = take(1)
            r_out, rc_ref, p_out, u_out, rb_out, pb_out, scal_out = take(7)
        else:
            scal_out, = take(1)
    ta, tf, bb, s1, hu, hd, hc = take(7)
    ta_s, ta_r, h_s, h_r, s1_s, s1_r, b_s, b_r, c_s, c_r = take(10)
    if mode != "first":
        q_ref, s2, s3, s2_s, s2_r, s3_s, s3_r = take(7)
    if mode != "last":
        hu2, hd2, hc2, k_s, k_r = take(5)
    me = lax.axis_index("swath")
    z = lax.axis_index("chan")
    chunk = table_ref.shape[1]

    def to_lat(d):
        return {"swath": lax.rem(me + d, n)}

    def to_lon(d):
        return {"chan": lax.rem(z + d, m)}

    def send(src, dst, ss, rs, dev):
        copy = pltpu.make_async_remote_copy(
            src_ref=src, dst_ref=dst, send_sem=ss, recv_sem=rs,
            device_id=dev, device_id_type=pl.DeviceIdType.MESH,
        )
        copy.start()
        return copy

    barrier = pltpu.get_barrier_semaphore()
    for d in range(1, n):
        pl.semaphore_signal(barrier, inc=1, device_id=to_lat(d), device_id_type=pl.DeviceIdType.MESH)
    for d in range(1, m):
        pl.semaphore_signal(barrier, inc=1, device_id=to_lon(d), device_id_type=pl.DeviceIdType.MESH)
    pl.semaphore_wait(barrier, n - 1 + m - 1)
    pending = []

    def halo(field, cols, up, down, side, ss, rs):
        copies = [
            send(field.at[LAT_DEV - 1], up, ss.at[0], rs.at[0], to_lat(1)),
            send(field.at[0], down, ss.at[1], rs.at[1], to_lat(n - 1)),
            send(cols.at[1], side.at[0], ss.at[2], rs.at[2], to_lon(1)),
            send(cols.at[0], side.at[1], ss.at[3], rs.at[3], to_lon(m - 1)),
        ]
        pending.extend(copies)
        return copies

    def landed(copies):
        for copy in copies:
            copy.wait_recv()

    halos = halo(g_ref, gc_ref, hu, hd, hc, h_s, h_r)
    parts = [
        send(table_ref.at[lax.rem(me + d, n)], ta.at[d], ta_s.at[d], ta_r.at[d], to_lat(d))
        for d in range(1, n)
    ]
    pending.extend(parts)
    smooth = smooth_ref[0:1, :]
    top_keep = (me > 0).astype(F32)
    bottom_keep = (me < n - 1).astype(F32)
    column = lax.broadcasted_iota(jnp.int32, (LON_DEV, LEV), 0)

    def stencil(field, i, above, below, side):
        mid = field[i]
        left = jnp.where(column == 0, side[0, pl.ds(i, 1), :], pltpu.roll(mid, 1, 0))
        right = jnp.where(
            column == LON_DEV - 1, side[1, pl.ds(i, 1), :], pltpu.roll(mid, LON_DEV - 1, 0)
        )
        return mid + smooth * (above + below + left + right - 4.0 * mid)

    def sweep(field, up, down, side, use, acc):
        acc = use(0, stencil(field, 0, up[...] * top_keep, field[1], side), acc)
        acc = lax.fori_loop(
            1,
            LAT_DEV - 1,
            lambda i, a: use(i, stencil(field, i, field[i - 1], field[i + 1], side), a),
            acc,
        )
        end = LAT_DEV - 1
        return use(end, stencil(field, end, field[end - 1], down[...] * bottom_keep, side), acc)

    def keep_columns(i, row):
        rc_ref[0, pl.ds(i, 1), :] = row[0:1]
        rc_ref[1, pl.ds(i, 1), :] = row[LON_DEV - 1 : LON_DEV]

    landed(halos)
    zero = jnp.zeros((LON_DEV, LEV), F32)
    if mode == "first":

        def use(i, row, acc):
            r_out[i] = row
            keep_columns(i, row)
            return acc + row * row

    else:

        def use(i, row, acc):
            p = p_ref[i]
            q = p + row
            q_ref[i] = q
            return acc + p * q

    s1[me] = fold(sweep(g_ref, hu, hd, hc, use, zero))
    ones = [send(s1.at[me], s1.at[me], s1_s.at[d], s1_r.at[d], to_lat(d)) for d in range(1, n)]
    pending.extend(ones)
    if mode == "first":
        second = halo(r_out, rc_ref, hu2, hd2, hc2, k_s, k_r)
    landed(parts)
    total = table_ref[me]
    for d in range(1, n):
        total = total + ta[d]
    landed(ones)
    scalar = s1[0]
    for j in range(1, n):
        scalar = scalar + s1[j]
    bb[z, 0:chunk] = total
    bb[z, chunk] = scalar
    across = [send(bb.at[z], bb.at[z], b_s.at[d], b_r.at[d], to_lon(d)) for d in range(1, m)]
    pending.extend(across)
    landed(across)
    merged = bb[0]
    for j in range(1, m):
        merged = merged + bb[j]
    tf[me] = merged[0:chunk]
    state_sum = jnp.full((8, LANES), jnp.sum(merged[chunk]), F32)
    gathers = [send(tf.at[me], tf.at[me], c_s.at[d], c_r.at[d], to_lat(d)) for d in range(1, n)]
    pending.extend(gathers)
    landed(gathers)

    def tab(j):
        return tf[j // chunk, j % chunk]

    def spread(tile):
        return jnp.full((8, LANES), jnp.sum(tile), F32)

    rz_bias = jnp.zeros((8, LANES), F32)
    rr_bias = jnp.zeros((8, LANES), F32)
    if mode == "first":
        for j in range(width):
            rb = tab(j)
            bp = tab(2 * width + j)
            diag = bp + tab(width + j)
            pb = rb / diag
            rb_out[j], bp_out[j], diag_out[j], pb_out[j] = rb, bp, diag, pb
            rz_bias = rz_bias + rb * pb
            rr_bias = rr_bias + rb * rb
        scal_out[0] = state_sum + spread(rz_bias)
        scal_out[1] = state_sum + spread(rr_bias)
        scal_out[2] = jnp.zeros((8, LANES), F32)
        landed(second)

        def use_u(i, row, acc):
            u_out[i] = row
            return acc

        sweep(r_out, hu2, hd2, hc2, use_u, 0)
    else:
        curve = jnp.zeros((8, LANES), F32)
        qbs = []
        for j in range(width):
            pb = pb_ref[j]
            curve = curve + pb * (bp_ref[j] * pb + tab(j))
        alpha = scal_ref[0] / (state_sum + spread(curve))
        line = alpha[0:1, :]

        def update(i, acc):
            row = r_ref[i] - line * q_ref[i]
            if mode == "middle":
                r_out[i] = row
                keep_columns(i, row)
            return acc + row * row

        s2[me] = fold(lax.fori_loop(0, LAT_DEV, update, zero))
        twos = [send(s2.at[me], s2.at[me], s2_s.at[d], s2_r.at[d], to_lat(d)) for d in range(1, n)]
        pending.extend(twos)
        if mode == "middle":
            second = halo(r_out, rc_ref, hu2, hd2, hc2, k_s, k_r)
        for j in range(width):
            pb = pb_ref[j]
            rb = rb_ref[j] - alpha * (bp_ref[j] * pb + tab(j))
            zb = rb / diag_ref[j]
            if mode == "middle":
                rb_out[j] = rb
            rz_bias = rz_bias + rb * zb
            rr_bias = rr_bias + rb * rb
        rz_bias, rr_bias = spread(rz_bias), spread(rr_bias)
        landed(twos)
        scalar = s2[0]
        for j in range(1, n):
            scalar = scalar + s2[j]
        s3[z] = scalar
        threes = [send(s3.at[z], s3.at[z], s3_s.at[d], s3_r.at[d], to_lon(d)) for d in range(1, m)]
        pending.extend(threes)
        landed(threes)
        scalar = s3[0]
        for j in range(1, m):
            scalar = scalar + s3[j]
        state_sum = spread(scalar)
        rz_new = state_sum + rz_bias
        scal_out[0] = rz_new
        scal_out[1] = state_sum + rr_bias
        scal_out[2] = alpha
        if mode == "middle":
            beta = rz_new / scal_ref[0]
            slope = beta[0:1, :]
            for j in range(width):
                pb_out[j] = rb_out[j] / diag_ref[j] + beta * pb_ref[j]
            landed(second)

            def use_u(i, row, acc):
                u_out[i] = row + slope * u_ref[i]
                p_out[i] = r_out[i] + slope * p_ref[i]
                return acc

            sweep(r_out, hu2, hd2, hc2, use_u, 0)
    for copy in pending:
        copy.wait_send()


VM = pl.BlockSpec(memory_space=pltpu.VMEM)
SM = pl.BlockSpec(memory_space=pltpu.SMEM)


def shaped(*shape):
    return jax.ShapeDtypeStruct(shape, F32)


def body(
    innovations,
    obs_precision,
    jacobian,
    predictors,
    obs_column,
    obs_channel,
    obs_count,
    smoothing,
    bias_precision,
):
    n = lax.axis_size("swath")
    m = lax.axis_size("chan")
    me = lax.axis_index("swath")
    z = lax.axis_index("chan")
    owned_width = bias_precision.shape[1]
    own = owned_width // LANES
    width = own * m
    blocks = owned_width * m // CH_BLOCK
    slots = obs_precision.shape[0]
    lines = slots // OBS_BLOCK
    grid_lines = lambda a: a.reshape(lines, OBS_BLOCK)
    cells = grid_lines(obs_column)
    line_rows = cells[:, 0] // LON_DEV
    own_bp = bias_precision.reshape(NPRED, own, LANES).transpose(1, 0, 2)
    own_bp = jnp.where(me == 0, own_bp, 0.0)
    bp_spread = lax.dynamic_update_slice(
        jnp.zeros((width, NPRED, LANES), F32), own_bp, (z * own, 0, 0)
    )
    common = (
        line_rows, obs_count, cells, grid_lines(obs_channel), grid_lines(obs_precision),
        predictors, jacobian,
    )
    field = shaped(LAT_DEV, LON_DEV, LEV)
    cols = shaped(2, LAT_DEV, LEV)
    tab = shaped(width, NPRED, LANES)
    scal = shaped(3, 8, LANES)
    smooth = smoothing.reshape(1, LEV)

    def local(init, *extra):
        used = (3 if init else 1) * width
        padded = -(-used // n) * n
        acc_rows = (4 if init else 2) * NPRED * blocks
        scratch = [pltpu.VMEM((acc_rows, CH_BLOCK), F32)]
        if not init:
            scratch += [
                pltpu.VMEM((LAT_DEV, 2 * LON_DEV, LEV), BF16),
                pltpu.VMEM((NPRED * blocks, CH_BLOCK), F32),
            ]
        out = pl.pallas_call(
            functools.partial(local_kernel, init, blocks),
            out_shape=(field, cols, shaped(padded, NPRED, LANES)),
            in_specs=[SM, SM] + [VM] * (len(common) - 2 + len(extra)),
            out_specs=(VM, VM, VM),
            scratch_shapes=scratch,
            compiler_params=pltpu.CompilerParams(vmem_limit_bytes=VMEM_LIMIT),
            name="local_first" if init else "local_next",
        )(*common, *extra)
        return out[0], out[1], out[2].reshape(n, padded // n, NPRED, LANES)

    def comm(mode, ident, outs, table, *args):
        chunk = table.shape[1]
        sem = lambda k: [pltpu.SemaphoreType.DMA((k,)), pltpu.SemaphoreType.DMA((k,))]
        vm = lambda *s: pltpu.VMEM(s, F32)
        scratch = [
            vm(n, chunk, NPRED, LANES), vm(n, chunk, NPRED, LANES), vm(m, chunk + 1, NPRED, LANES),
            vm(n, 8, LANES), vm(LON_DEV, LEV), vm(LON_DEV, LEV), vm(2, LAT_DEV, LEV),
        ] + sem(n) + sem(4) + sem(n) + sem(m) + sem(n)
        if mode != "first":
            scratch += [vm(LAT_DEV, LON_DEV, LEV), vm(n, 8, LANES), vm(m, 8, LANES)] + sem(n) + sem(m)
        if mode != "last":
            scratch += [vm(LON_DEV, LEV), vm(LON_DEV, LEV), vm(2, LAT_DEV, LEV)] + sem(4)
        return pl.pallas_call(
            functools.partial(comm_kernel, n, m, width, mode),
            out_shape=outs,
            in_specs=[VM] * (4 + len(args)),
            out_specs=jax.tree.map(lambda _: VM, outs),
            scratch_shapes=scratch,
            compiler_params=pltpu.CompilerParams(
                collective_id=ident, has_side_effects=True, vmem_limit_bytes=VMEM_LIMIT
            ),
            name="comm_" + mode,
        )(smooth, *grads, table, *args)

    g, gc, table = local(True, grid_lines(innovations), bp_spread)
    grads = (g, gc)
    r, _, u, rb, diag, bp, pb, sc = comm(
        "first", 0, (field, cols, field, tab, tab, tab, tab, scal), table
    )
    p = r
    record = [sc[1, 0, 0]]
    state = None
    bias = None
    for turn in range(ITERS):
        g, gc, table = local(False, u, pb)
        grads = (g, gc)
        args = (p, r, pb, rb, diag, bp, sc)
        old_p, old_pb = p, pb
        if turn < ITERS - 1:
            r, _, p, u, rb, pb, sc = comm(
                "middle", 1 + turn, (field, cols, field, field, tab, tab, scal), table, *args, u
            )
        else:
            (sc,) = comm("last", 1 + turn, (scal,), table, *args)
        length = sc[2, 0, 0]
        record.append(sc[1, 0, 0])
        mine = lax.dynamic_slice(old_pb, (z * own, 0, 0), (own, NPRED, LANES))
        state = length * old_p if state is None else state + length * old_p
        bias = length * mine if bias is None else bias + length * mine
    bias = bias.transpose(1, 0, 2).reshape(NPRED, owned_width)
    return (state, bias, jnp.sqrt(jnp.stack(record)))


def solution(mesh):
    placed = (
        P(("swath", "chan")),
        P(("swath", "chan")),
        P(("swath", "chan"), None),
        P(None, ("swath", "chan")),
        P(("swath", "chan")),
        P(("swath", "chan")),
        P("swath", "chan"),
        P(),
        P(None, "chan"),
    )
    return jax.shard_map(
        body,
        mesh=mesh,
        in_specs=placed,
        out_specs=(P("swath", "chan", None), P(None, "chan"), P()),
        check_vma=False,
    )
```

```python
import functools

import jax
import jax.numpy as jnp
from jax import lax
from jax.experimental import pallas as pl
from jax.experimental.pallas import tpu as pltpu
from jax.sharding import PartitionSpec as P

LEV = 128
NPRED = 8
CH_BLOCK = 256
OBS_BLOCK = 128
LAT_DEV = 32
LON_DEV = 64
ITERS = 2
LINES = 8
LANES = 128
F32 = jnp.float32
BF16 = jnp.bfloat16
NT = (((1,), (1,)), ((), ()))
VMEM_LIMIT = 24 * 1024 * 1024


def halves(value):
    high = value.astype(BF16)
    return high, (value - high.astype(F32)).astype(BF16)


def local_kernel(init, blocks, rows_ref, count_ref, cell_ref, chan_ref, prec_ref, pred_ref, jac_ref, *refs):
    if init:
        innov_ref, field_ref, cols_ref, table_ref, acc_ref = refs
    else:
        u_ref, coef_ref, field_ref, cols_ref, table_ref, acc_ref, split_ref, flat_ref = refs
    n_lines = cell_ref.shape[0]
    rows_tab = NPRED * blocks
    tables = 2 if init else 1
    count = count_ref[0, 0]
    field_ref[...] = jnp.zeros_like(field_ref)
    acc_ref[...] = jnp.zeros_like(acc_ref)

    if not init:
        def split_row(i, carry):
            high, low = halves(u_ref[i])
            split_ref[i] = jnp.concatenate([high, low], axis=0)
            return carry

        lax.fori_loop(0, LAT_DEV, split_row, 0)
        for b in range(blocks):
            for h in range(CH_BLOCK // LANES):
                block = coef_ref[b * (CH_BLOCK // LANES) + h]
                flat_ref[b * NPRED : (b + 1) * NPRED, h * LANES : (h + 1) * LANES] = block
        high, low = halves(flat_ref[...])
        coef2 = jnp.concatenate([high, low], axis=0)

    iota_col = lax.broadcasted_iota(jnp.int32, (LON_DEV, OBS_BLOCK), 0)
    iota_ch = lax.broadcasted_iota(jnp.int32, (CH_BLOCK, OBS_BLOCK), 0)
    iota_obs = lax.broadcasted_iota(jnp.int32, (1, OBS_BLOCK), 1)

    def step(it, carry):
        base = pl.multiple_of(it * LINES, LINES)
        cells = cell_ref[pl.ds(base, LINES), :]
        chans = chan_ref[pl.ds(base, LINES), :]
        precs = prec_ref[pl.ds(base, LINES), :]
        if init:
            innovs = innov_ref[pl.ds(base, LINES), :]
        hots, his, masks, weights, preds, jacs, rows = [], [], [], [], [], [], []
        for l in range(LINES):
            ch = chans[l : l + 1, :]
            hots.append(jnp.where(iota_ch == ch % CH_BLOCK, 1.0, 0.0).astype(BF16))
            his.append(jnp.broadcast_to(ch // CH_BLOCK, (NPRED, OBS_BLOCK)))
            masks.append(iota_col == cells[l : l + 1, :] % LON_DEV)
            slot = (base + l) * OBS_BLOCK + iota_obs
            weights.append(jnp.where(slot < count, precs[l : l + 1, :], 0.0))
            start = pl.multiple_of((base + l) * OBS_BLOCK, OBS_BLOCK)
            preds.append(pred_ref[:, pl.ds(start, OBS_BLOCK)])
            jacs.append(jac_ref[pl.ds(start, OBS_BLOCK), :])
            rows.append(rows_ref[base + l])
        values = []
        if init:
            for l in range(LINES):
                values.append(weights[l] * innovs[l : l + 1, :])
        else:
            looked = []
            for l in range(0, LINES, 2):
                pair = jnp.concatenate(hots[l : l + 2], axis=1)
                mid = jnp.dot(coef2, pair, preferred_element_type=F32)
                for j in range(2):
                    total = jnp.zeros((NPRED, OBS_BLOCK), F32)
                    lanes = slice(j * OBS_BLOCK, (j + 1) * OBS_BLOCK)
                    for b in range(blocks):
                        top = mid[b * NPRED : (b + 1) * NPRED, lanes]
                        low = mid[rows_tab + b * NPRED : rows_tab + (b + 1) * NPRED, lanes]
                        total = total + jnp.where(his[l + j] == b, top + low, 0.0)
                    looked.append(jnp.sum(total * preds[l + j], axis=0, keepdims=True))
            for l in range(LINES):
                prod = lax.dot_general(split_ref[rows[l]], jacs[l], NT, preferred_element_type=F32)
                both = prod[:LON_DEV] + prod[LON_DEV:]
                seen = jnp.sum(jnp.where(masks[l], both, 0.0), axis=0, keepdims=True)
                values.append(weights[l] * (seen + looked[l]))
        outs = []
        for l in range(LINES):
            high, low = halves(jnp.where(masks[l], values[l], 0.0))
            spread = jnp.concatenate([high, low], axis=0)
            out = jnp.dot(spread, jacs[l], preferred_element_type=F32)
            outs.append(out[:LON_DEV] + out[LON_DEV:])
        for l in range(LINES):
            field_ref[rows[l]] += outs[l]
        lefts = []
        for l in range(LINES):
            pieces = []
            terms = [preds[l] * values[l]]
            if init:
                terms.append(preds[l] * preds[l] * weights[l])
            for term in terms:
                wide = jnp.concatenate(
                    [jnp.where(his[l] == b, term, 0.0) for b in range(blocks)], axis=0
                )
                pieces.extend(halves(wide))
            lefts.append(jnp.concatenate(pieces, axis=0))
        left = jnp.concatenate(lefts, axis=1)
        hot = jnp.concatenate(hots, axis=1)
        acc_ref[...] += lax.dot_general(left, hot, NT, preferred_element_type=F32)
        return carry

    lax.fori_loop(0, n_lines // LINES, step, 0)
    per = CH_BLOCK // LANES
    used = tables * blocks * per
    for t in range(tables):
        for b in range(blocks):
            for h in range(per):
                top = t * 2 * rows_tab + b * NPRED
                low = top + rows_tab
                lanes = slice(h * LANES, (h + 1) * LANES)
                table_ref[(t * blocks + b) * per + h] = (
                    acc_ref[top : top + NPRED, lanes] + acc_ref[low : low + NPRED, lanes]
                )
    if table_ref.shape[0] > used:
        table_ref[used:] = jnp.zeros((table_ref.shape[0] - used, NPRED, LANES), F32)

    def column(i, carry):
        cols_ref[0, pl.ds(i, 1), :] = field_ref[i, 0:1, :]
        cols_ref[1, pl.ds(i, 1), :] = field_ref[i, LON_DEV - 1 : LON_DEV, :]
        return carry

    lax.fori_loop(0, LAT_DEV, column, 0)


def fold(value):
    total = value[0:8]
    for i in range(1, value.shape[0] // 8):
        total = total + value[8 * i : 8 * i + 8]
    return total


def comm_kernel(n, m, width, mode, turn, *refs):
    refs = list(refs)
    take = lambda k: [refs.pop(0) for _ in range(k)]
    smooth_ref, g_ref, gc_ref, table_ref = take(4)
    if mode == "first":
        own_ref, = take(1)
        r_out, rc_ref, u_out, rb_out, diag_out, bp_out, pb_out, scal_out = take(8)
    else:
        p_ref, r_ref, pb_ref, rb_ref, diag_ref, bp_ref, scal_ref = take(7)
        if mode == "middle":
            u_ref, = take(1)
            r_out, rc_ref, p_out, u_out, rb_out, pb_out, scal_out, x_out = take(8)
        else:
            xb_ref, = take(1)
            scal_out, norms_out, bias_out = take(3)
    ta, tf, bb, s1, sc, hu, hd, hc = take(8)
    ta_s, ta_r, h_s, h_r, s1_s, s1_r, b_s, b_r, c_s, c_r, sc_s, sc_r = take(12)
    if mode == "first":
        own_all, o_s, o_r = take(3)
    if mode != "first":
        q_ref, s2, s3, s2_s, s2_r, s3_s, s3_r = take(7)
    if mode != "last":
        hu2, hd2, hc2, k_s, k_r = take(5)
    me = lax.axis_index("swath")
    z = lax.axis_index("chan")
    chunk = table_ref.shape[1]

    def to_lat(d):
        return {"swath": lax.rem(me + d, n)}

    def to_lon(d):
        return {"chan": lax.rem(z + d, m)}

    def send(src, dst, ss, rs, dev):
        copy = pltpu.make_async_remote_copy(
            src_ref=src, dst_ref=dst, send_sem=ss, recv_sem=rs,
            device_id=dev, device_id_type=pl.DeviceIdType.MESH,
        )
        copy.start()
        return copy

    barrier = pltpu.get_barrier_semaphore()
    for d in range(1, n):
        pl.semaphore_signal(barrier, inc=1, device_id=to_lat(d), device_id_type=pl.DeviceIdType.MESH)
    for d in range(1, m):
        pl.semaphore_signal(barrier, inc=1, device_id=to_lon(d), device_id_type=pl.DeviceIdType.MESH)
    pl.semaphore_wait(barrier, n - 1 + m - 1)
    pending = []

    def halo(field, cols, up, down, side, ss, rs):
        copies = [
            send(field.at[LAT_DEV - 1], up, ss.at[0], rs.at[0], to_lat(1)),
            send(field.at[0], down, ss.at[1], rs.at[1], to_lat(n - 1)),
            send(cols.at[1], side.at[0], ss.at[2], rs.at[2], to_lon(1)),
            send(cols.at[0], side.at[1], ss.at[3], rs.at[3], to_lon(m - 1)),
        ]
        pending.extend(copies)
        return copies

    def landed(copies):
        for copy in copies:
            copy.wait_recv()

    halos = halo(g_ref, gc_ref, hu, hd, hc, h_s, h_r)
    if mode == "first":
        own = own_ref.shape[1] // LANES
        for j in range(own):
            own_all[z, j] = own_ref[:, j * LANES : (j + 1) * LANES]
        owners = [send(own_all.at[z], own_all.at[z], o_s.at[d], o_r.at[d], to_lon(d)) for d in range(1, m)]
        pending.extend(owners)
    parts = [
        send(table_ref.at[lax.rem(me + d, n)], ta.at[d], ta_s.at[d], ta_r.at[d], to_lat(d))
        for d in range(1, n)
    ]
    pending.extend(parts)
    smooth = smooth_ref[0:1, :]
    top_keep = (me > 0).astype(F32)
    bottom_keep = (me < n - 1).astype(F32)
    column = lax.broadcasted_iota(jnp.int32, (LON_DEV, LEV), 0)

    def stencil(field, i, above, below, side):
        mid = field[i]
        left = jnp.where(column == 0, side[0, pl.ds(i, 1), :], pltpu.roll(mid, 1, 0))
        right = jnp.where(
            column == LON_DEV - 1, side[1, pl.ds(i, 1), :], pltpu.roll(mid, LON_DEV - 1, 0)
        )
        return mid + smooth * (above + below + left + right - 4.0 * mid)

    def sweep(field, up, down, side, use, acc):
        acc = use(0, stencil(field, 0, up[...] * top_keep, field[1], side), acc)
        inner = LAT_DEV - 2
        group = next(k for k in (5, 4, 3, 2, 1) if inner % k == 0)

        def rows(it, a):
            for k in range(group):
                i = 1 + it * group + k
                a = use(i, stencil(field, i, field[i - 1], field[i + 1], side), a)
            return a

        acc = lax.fori_loop(0, inner // group, rows, acc)
        end = LAT_DEV - 1
        return use(end, stencil(field, end, field[end - 1], down[...] * bottom_keep, side), acc)

    def keep_columns(i, row):
        rc_ref[0, pl.ds(i, 1), :] = row[0:1]
        rc_ref[1, pl.ds(i, 1), :] = row[LON_DEV - 1 : LON_DEV]

    zero = jnp.zeros((LON_DEV, LEV), F32)
    if mode == "first":

        def use(i, row, acc):
            r_out[i] = row
            keep_columns(i, row)
            return acc + row * row

    else:

        def use(i, row, acc):
            p = p_ref[i]
            q = p + row
            q_ref[i] = q
            return acc + p * q

    def scatter_sum():
        landed(parts)
        total = table_ref[me]
        for d in range(1, n):
            total = total + ta[d]
        bb[z] = total
        across = [send(bb.at[z], bb.at[z], b_s.at[d], b_r.at[d], to_lon(d)) for d in range(1, m)]
        pending.extend(across)
        return across

    def everywhere(buf, tile, ss, rs):
        buf[me] = tile
        copies = [send(buf.at[me], buf.at[me], ss.at[d], rs.at[d], to_lat(d)) for d in range(1, n)]
        pending.extend(copies)
        return copies

    def summed(buf, count):
        total = buf[0]
        for j in range(1, count):
            total = total + buf[j]
        return total

    def along_lon(buf, tile, ss, rs):
        buf[z] = tile
        copies = [send(buf.at[z], buf.at[z], ss.at[d], rs.at[d], to_lon(d)) for d in range(1, m)]
        pending.extend(copies)
        return copies

    if mode != "first":
        across = scatter_sum()
    landed(halos)
    ones = everywhere(s1, fold(sweep(g_ref, hu, hd, hc, use, zero)), s1_s, s1_r)
    if mode == "first":
        second = halo(r_out, rc_ref, hu2, hd2, hc2, k_s, k_r)
        across = scatter_sum()
    landed(across)
    gathers = everywhere(tf, summed(bb, m), c_s, c_r)
    landed(ones)
    crossing = along_lon(sc, summed(s1, n), sc_s, sc_r)
    landed(gathers)

    def tab(j):
        return tf[j // chunk, j % chunk]

    def spread(tile):
        return jnp.full((8, LANES), jnp.sum(tile), F32)

    rz_bias = jnp.zeros((8, LANES), F32)
    rr_bias = jnp.zeros((8, LANES), F32)
    if mode == "first":
        landed(owners)
        for j in range(width):
            rb = tab(j)
            bp = own_all[j // own, j % own]
            diag = bp + tab(width + j)
            pb = rb / diag
            rb_out[j], bp_out[j], diag_out[j], pb_out[j] = rb, bp, diag, pb
            rz_bias = rz_bias + rb * pb
            rr_bias = rr_bias + rb * rb
        rz_bias, rr_bias = spread(rz_bias), spread(rr_bias)
        landed(crossing)
        state_sum = spread(summed(sc, m))
        scal_out[...] = jnp.zeros(scal_out.shape, F32)
        scal_out[0] = state_sum + rz_bias
        scal_out[1] = state_sum + rr_bias
        landed(second)

        def use_u(i, row, acc):
            u_out[i] = row
            return acc

        sweep(r_out, hu2, hd2, hc2, use_u, 0)
    else:
        curve = jnp.zeros((8, LANES), F32)
        for j in range(width):
            pb = pb_ref[j]
            curve = curve + pb * (bp_ref[j] * pb + tab(j))
        curve = spread(curve)
        landed(crossing)
        alpha = scal_ref[0] / (spread(summed(sc, m)) + curve)
        line = alpha[0:1, :]

        def update(it, acc):
            for k in range(4):
                i = it * 4 + k
                row = r_ref[i] - line * q_ref[i]
                if mode == "middle":
                    r_out[i] = row
                    keep_columns(i, row)
                acc = acc + row * row
            return acc

        twos = everywhere(s2, fold(lax.fori_loop(0, LAT_DEV // 4, update, zero)), s2_s, s2_r)
        if mode == "middle":
            second = halo(r_out, rc_ref, hu2, hd2, hc2, k_s, k_r)
        for j in range(width):
            pb = pb_ref[j]
            rb = rb_ref[j] - alpha * (bp_ref[j] * pb + tab(j))
            zb = rb / diag_ref[j]
            if mode == "middle":
                rb_out[j] = rb
                x_out[j] = alpha * pb
            rz_bias = rz_bias + rb * zb
            rr_bias = rr_bias + rb * rb
        rz_bias, rr_bias = spread(rz_bias), spread(rr_bias)
        landed(twos)
        threes = along_lon(s3, summed(s2, n), s3_s, s3_r)
        if mode == "last":
            own = bias_out.shape[1] // LANES
            for j in range(own):
                bias_out[:, j * LANES : (j + 1) * LANES] = (
                    xb_ref[z * own + j] + alpha * pb_ref[z * own + j]
                )
        landed(threes)
        state_sum = spread(summed(s3, m))
        rz_new = state_sum + rz_bias
        scal_out[...] = scal_ref[...]
        scal_out[0] = rz_new
        scal_out[1 + turn] = state_sum + rr_bias
        scal_out[1 + ITERS + turn] = alpha
        if mode == "last":
            lane = lax.broadcasted_iota(jnp.int32, (8, LANES), 1)
            norms = jnp.zeros((8, LANES), F32)
            for j in range(ITERS + 1):
                norms = jnp.where(lane == j, scal_out[1 + j], norms)
            norms_out[...] = jnp.sqrt(norms)
        if mode == "middle":
            beta = rz_new / scal_ref[0]
            slope = beta[0:1, :]
            for j in range(width):
                pb_out[j] = rb_out[j] / diag_ref[j] + beta * pb_ref[j]
            landed(second)

            def use_u(i, row, acc):
                u_out[i] = row + slope * u_ref[i]
                p_out[i] = r_out[i] + slope * p_ref[i]
                return acc

            sweep(r_out, hu2, hd2, hc2, use_u, 0)
    for copy in pending:
        copy.wait_send()


VM = pl.BlockSpec(memory_space=pltpu.VMEM)
SM = pl.BlockSpec(memory_space=pltpu.SMEM)


def shaped(*shape):
    return jax.ShapeDtypeStruct(shape, F32)


def body(
    innovations,
    obs_precision,
    jacobian,
    predictors,
    obs_column,
    obs_channel,
    obs_count,
    smoothing,
    bias_precision,
):
    n = lax.axis_size("swath")
    m = lax.axis_size("chan")
    owned_width = bias_precision.shape[1]
    own = owned_width // LANES
    width = own * m
    blocks = owned_width * m // CH_BLOCK
    slots = obs_precision.shape[0]
    lines = slots // OBS_BLOCK
    grid_lines = lambda a: a.reshape(lines, OBS_BLOCK)
    cells = grid_lines(obs_column)
    line_rows = cells[:, 0] // LON_DEV
    common = (
        line_rows, obs_count, cells, grid_lines(obs_channel), grid_lines(obs_precision),
        predictors, jacobian,
    )
    field = shaped(LAT_DEV, LON_DEV, LEV)
    cols = shaped(2, LAT_DEV, LEV)
    tab = shaped(width, NPRED, LANES)
    scal = shaped(2 + 2 * ITERS, 8, LANES)
    smooth = smoothing.reshape(1, LEV)

    def local(init, *extra):
        used = (2 if init else 1) * width
        padded = -(-used // n) * n
        acc_rows = (4 if init else 2) * NPRED * blocks
        scratch = [pltpu.VMEM((acc_rows, CH_BLOCK), F32)]
        if not init:
            scratch += [
                pltpu.VMEM((LAT_DEV, 2 * LON_DEV, LEV), BF16),
                pltpu.VMEM((NPRED * blocks, CH_BLOCK), F32),
            ]
        out = pl.pallas_call(
            functools.partial(local_kernel, init, blocks),
            out_shape=(field, cols, shaped(padded, NPRED, LANES)),
            in_specs=[SM, SM] + [VM] * (len(common) - 2 + len(extra)),
            out_specs=(VM, VM, VM),
            scratch_shapes=scratch,
            compiler_params=pltpu.CompilerParams(vmem_limit_bytes=VMEM_LIMIT),
            name="local_first" if init else "local_next",
        )(*common, *extra)
        return out[0], out[1], out[2].reshape(n, padded // n, NPRED, LANES)

    def comm(mode, ident, outs, table, *args):
        chunk = table.shape[1]
        sem = lambda k: [pltpu.SemaphoreType.DMA((k,)), pltpu.SemaphoreType.DMA((k,))]
        vm = lambda *s: pltpu.VMEM(s, F32)
        scratch = [
            vm(n, chunk, NPRED, LANES), vm(n, chunk, NPRED, LANES), vm(m, chunk, NPRED, LANES),
            vm(n, 8, LANES), vm(m, 8, LANES), vm(LON_DEV, LEV), vm(LON_DEV, LEV), vm(2, LAT_DEV, LEV),
        ] + sem(n) + sem(4) + sem(n) + sem(m) + sem(n) + sem(m)
        if mode == "first":
            scratch += [vm(m, own, NPRED, LANES)] + sem(m)
        if mode != "first":
            scratch += [vm(LAT_DEV, LON_DEV, LEV), vm(n, 8, LANES), vm(m, 8, LANES)] + sem(n) + sem(m)
        if mode != "last":
            scratch += [vm(LON_DEV, LEV), vm(LON_DEV, LEV), vm(2, LAT_DEV, LEV)] + sem(4)
        return pl.pallas_call(
            functools.partial(comm_kernel, n, m, width, mode, ident),
            out_shape=outs,
            in_specs=[VM] * (4 + len(args)),
            out_specs=jax.tree.map(lambda _: VM, outs),
            scratch_shapes=scratch,
            compiler_params=pltpu.CompilerParams(
                collective_id=ident, has_side_effects=True, vmem_limit_bytes=VMEM_LIMIT
            ),
            name="comm_" + mode,
        )(smooth, *grads, table, *args)

    g, gc, table = local(True, grid_lines(innovations))
    grads = (g, gc)
    r, _, u, rb, diag, bp, pb, sc = comm(
        "first", 0, (field, cols, field, tab, tab, tab, tab, scal), table, bias_precision
    )
    p = r
    state = None
    total = None
    for turn in range(1, ITERS + 1):
        g, gc, table = local(False, u, pb)
        grads = (g, gc)
        args = (p, r, pb, rb, diag, bp, sc)
        old_p = p
        if turn < ITERS:
            outs = (field, cols, field, field, tab, tab, scal, tab)
            r, _, p, u, rb, pb, sc, total = comm("middle", turn, outs, table, *args, u)
        else:
            outs = (scal, shaped(8, LANES), shaped(NPRED, owned_width))
            sc, norms, bias = comm("last", turn, outs, table, *args, total)
        length = sc[1 + ITERS + turn, 0]
        state = length * old_p if state is None else state + length * old_p
    return (state, bias, norms[0, : ITERS + 1])


def solution(mesh):
    placed = (
        P(("swath", "chan")),
        P(("swath", "chan")),
        P(("swath", "chan"), None),
        P(None, ("swath", "chan")),
        P(("swath", "chan")),
        P(("swath", "chan")),
        P("swath", "chan"),
        P(),
        P(None, "chan"),
    )
    return jax.shard_map(
        body,
        mesh=mesh,
        in_specs=placed,
        out_specs=(P("swath", "chan", None), P(None, "chan"), P()),
        check_vma=False,
    )
```

```python
import functools

import jax
import jax.numpy as jnp
from jax import lax
from jax.experimental import pallas as pl
from jax.experimental.pallas import tpu as pltpu
from jax.sharding import PartitionSpec as P

LEV = 128
NPRED = 8
CH_BLOCK = 256
OBS_BLOCK = 128
LAT_DEV = 32
LON_DEV = 64
ITERS = 2
LINES = 8
LANES = 128
F32 = jnp.float32
BF16 = jnp.bfloat16
NT = (((1,), (1,)), ((), ()))
VMEM_LIMIT = 24 * 1024 * 1024


def halves(value):
    high = value.astype(BF16)
    return high, (value - high.astype(F32)).astype(BF16)


def local_kernel(init, blocks, rows_ref, count_ref, cell_ref, chan_ref, prec_ref, pred_ref, jac_ref, *refs):
    if init:
        innov_ref, field_ref, cols_ref, table_ref, acc_ref = refs
    else:
        u_ref, coef_ref, field_ref, cols_ref, table_ref, acc_ref, split_ref, flat_ref = refs
    n_lines = cell_ref.shape[0]
    rows_tab = NPRED * blocks
    tables = 2 if init else 1
    count = count_ref[0, 0]
    field_ref[...] = jnp.zeros_like(field_ref)
    acc_ref[...] = jnp.zeros_like(acc_ref)

    if not init:
        def split_row(i, carry):
            high, low = halves(u_ref[i])
            split_ref[i] = jnp.concatenate([high, low], axis=1)
            return carry

        lax.fori_loop(0, LAT_DEV, split_row, 0)
        for b in range(blocks):
            for h in range(CH_BLOCK // LANES):
                block = coef_ref[b * (CH_BLOCK // LANES) + h]
                flat_ref[b * NPRED : (b + 1) * NPRED, h * LANES : (h + 1) * LANES] = block
        high, low = halves(flat_ref[...])
        coef2 = jnp.concatenate([high, low], axis=1)

    iota_col = lax.broadcasted_iota(jnp.int32, (LON_DEV, OBS_BLOCK), 0)
    iota_ch = lax.broadcasted_iota(jnp.int32, (CH_BLOCK, OBS_BLOCK), 0)
    iota_obs = lax.broadcasted_iota(jnp.int32, (1, OBS_BLOCK), 1)

    def step(it, carry):
        base = pl.multiple_of(it * LINES, LINES)
        cells = cell_ref[pl.ds(base, LINES), :]
        chans = chan_ref[pl.ds(base, LINES), :]
        precs = prec_ref[pl.ds(base, LINES), :]
        if init:
            innovs = innov_ref[pl.ds(base, LINES), :]
        hots, his, masks, weights, preds, jacs, rows = [], [], [], [], [], [], []
        for l in range(LINES):
            ch = chans[l : l + 1, :]
            hots.append(jnp.where(iota_ch == ch % CH_BLOCK, 1.0, 0.0).astype(BF16))
            his.append(jnp.broadcast_to(ch // CH_BLOCK, (NPRED, OBS_BLOCK)))
            masks.append(iota_col == cells[l : l + 1, :] % LON_DEV)
            slot = (base + l) * OBS_BLOCK + iota_obs
            weights.append(jnp.where(slot < count, precs[l : l + 1, :], 0.0))
            start = pl.multiple_of((base + l) * OBS_BLOCK, OBS_BLOCK)
            preds.append(pred_ref[:, pl.ds(start, OBS_BLOCK)])
            jacs.append(jac_ref[pl.ds(start, OBS_BLOCK), :])
            rows.append(rows_ref[base + l])
        values = []
        if init:
            for l in range(LINES):
                values.append(weights[l] * innovs[l : l + 1, :])
        else:
            looked = []
            for l in range(0, LINES, 2):
                pair = jnp.concatenate(hots[l : l + 2], axis=1)
                mid = jnp.dot(
                    coef2, jnp.concatenate([pair, pair], axis=0), preferred_element_type=F32
                )
                for j in range(2):
                    total = jnp.zeros((NPRED, OBS_BLOCK), F32)
                    lanes = slice(j * OBS_BLOCK, (j + 1) * OBS_BLOCK)
                    for b in range(blocks):
                        top = mid[b * NPRED : (b + 1) * NPRED, lanes]
                        total = total + jnp.where(his[l + j] == b, top, 0.0)
                    looked.append(jnp.sum(total * preds[l + j], axis=0, keepdims=True))
            for l in range(LINES):
                twice = jnp.concatenate([jacs[l], jacs[l]], axis=1)
                both = lax.dot_general(split_ref[rows[l]], twice, NT, preferred_element_type=F32)
                seen = jnp.sum(jnp.where(masks[l], both, 0.0), axis=0, keepdims=True)
                values.append(weights[l] * (seen + looked[l]))
        outs = []
        for l in range(LINES):
            high, low = halves(jnp.where(masks[l], values[l], 0.0))
            spread = jnp.concatenate([high, low], axis=1)
            twice = jnp.concatenate([jacs[l], jacs[l]], axis=0)
            outs.append(jnp.dot(spread, twice, preferred_element_type=F32))
        for l in range(LINES):
            field_ref[rows[l]] += outs[l]
        lefts, rights = [], []
        for l in range(LINES):
            highs, lows = [], []
            terms = [preds[l] * values[l]]
            if init:
                terms.append(preds[l] * preds[l] * weights[l])
            for term in terms:
                wide = jnp.concatenate(
                    [jnp.where(his[l] == b, term, 0.0) for b in range(blocks)], axis=0
                )
                high, low = halves(wide)
                highs.append(high)
                lows.append(low)
            lefts.append(jnp.concatenate(highs, axis=0))
            rights.append(jnp.concatenate(lows, axis=0))
        left = jnp.concatenate(lefts + rights, axis=1)
        hot = jnp.concatenate(hots + hots, axis=1)
        acc_ref[...] += lax.dot_general(left, hot, NT, preferred_element_type=F32)
        return carry

    lax.fori_loop(0, n_lines // LINES, step, 0)
    per = CH_BLOCK // LANES
    used = tables * blocks * per
    for t in range(tables):
        for b in range(blocks):
            for h in range(per):
                top = t * rows_tab + b * NPRED
                lanes = slice(h * LANES, (h + 1) * LANES)
                table_ref[(t * blocks + b) * per + h] = acc_ref[top : top + NPRED, lanes]
    if table_ref.shape[0] > used:
        table_ref[used:] = jnp.zeros((table_ref.shape[0] - used, NPRED, LANES), F32)

    def column(i, carry):
        cols_ref[0, pl.ds(i, 1), :] = field_ref[i, 0:1, :]
        cols_ref[1, pl.ds(i, 1), :] = field_ref[i, LON_DEV - 1 : LON_DEV, :]
        return carry

    lax.fori_loop(0, LAT_DEV, column, 0)


def fold(value):
    total = value[0:8]
    for i in range(1, value.shape[0] // 8):
        total = total + value[8 * i : 8 * i + 8]
    return total


def comm_kernel(n, m, width, mode, turn, *refs):
    refs = list(refs)
    take = lambda k: [refs.pop(0) for _ in range(k)]
    smooth_ref, g_ref, gc_ref, table_ref = take(4)
    if mode == "first":
        own_ref, = take(1)
        r_out, rc_ref, u_out, rb_out, diag_out, bp_out, pb_out, scal_out = take(8)
    else:
        p_ref, r_ref, pb_ref, rb_ref, diag_ref, bp_ref, scal_ref = take(7)
        if mode == "middle":
            u_ref, = take(1)
            r_out, rc_ref, p_out, u_out, rb_out, pb_out, scal_out, x_out = take(8)
        else:
            xb_ref, = take(1)
            scal_out, norms_out, bias_out = take(3)
    ta, tf, bb, s1, sc, hu, hd, hc = take(8)
    ta_s, ta_r, h_s, h_r, s1_s, s1_r, b_s, b_r, c_s, c_r, sc_s, sc_r = take(12)
    if mode == "first":
        own_all, o_s, o_r = take(3)
    if mode != "first":
        q_ref, s2, s3, s2_s, s2_r, s3_s, s3_r = take(7)
    if mode != "last":
        hu2, hd2, hc2, k_s, k_r = take(5)
    me = lax.axis_index("swath")
    z = lax.axis_index("chan")
    chunk = table_ref.shape[1]

    def to_lat(d):
        return {"swath": lax.rem(me + d, n)}

    def to_lon(d):
        return {"chan": lax.rem(z + d, m)}

    def send(src, dst, ss, rs, dev):
        copy = pltpu.make_async_remote_copy(
            src_ref=src, dst_ref=dst, send_sem=ss, recv_sem=rs,
            device_id=dev, device_id_type=pl.DeviceIdType.MESH,
        )
        copy.start()
        return copy

    barrier = pltpu.get_barrier_semaphore()
    for d in range(1, n):
        pl.semaphore_signal(barrier, inc=1, device_id=to_lat(d), device_id_type=pl.DeviceIdType.MESH)
    for d in range(1, m):
        pl.semaphore_signal(barrier, inc=1, device_id=to_lon(d), device_id_type=pl.DeviceIdType.MESH)
    pl.semaphore_wait(barrier, n - 1 + m - 1)
    pending = []

    def halo(field, cols, up, down, side, ss, rs):
        copies = [
            send(field.at[LAT_DEV - 1], up, ss.at[0], rs.at[0], to_lat(1)),
            send(field.at[0], down, ss.at[1], rs.at[1], to_lat(n - 1)),
            send(cols.at[1], side.at[0], ss.at[2], rs.at[2], to_lon(1)),
            send(cols.at[0], side.at[1], ss.at[3], rs.at[3], to_lon(m - 1)),
        ]
        pending.extend(copies)
        return copies

    def landed(copies):
        for copy in copies:
            copy.wait_recv()

    halos = halo(g_ref, gc_ref, hu, hd, hc, h_s, h_r)
    if mode == "first":
        own = own_ref.shape[1] // LANES
        for j in range(own):
            own_all[z, j] = own_ref[:, j * LANES : (j + 1) * LANES]
        owners = [send(own_all.at[z], own_all.at[z], o_s.at[d], o_r.at[d], to_lon(d)) for d in range(1, m)]
        pending.extend(owners)
    parts = [
        send(table_ref.at[lax.rem(me + d, n)], ta.at[d], ta_s.at[d], ta_r.at[d], to_lat(d))
        for d in range(1, n)
    ]
    pending.extend(parts)
    smooth = smooth_ref[0:1, :]
    top_keep = (me > 0).astype(F32)
    bottom_keep = (me < n - 1).astype(F32)
    column = lax.broadcasted_iota(jnp.int32, (LON_DEV, LEV), 0)

    def stencil(field, i, above, below, side):
        mid = field[i]
        left = jnp.where(column == 0, side[0, pl.ds(i, 1), :], pltpu.roll(mid, 1, 0))
        right = jnp.where(
            column == LON_DEV - 1, side[1, pl.ds(i, 1), :], pltpu.roll(mid, LON_DEV - 1, 0)
        )
        return mid + smooth * (above + below + left + right - 4.0 * mid)

    def sweep(field, up, down, side, use, acc):
        acc = use(0, stencil(field, 0, up[...] * top_keep, field[1], side), acc)
        inner = LAT_DEV - 2
        group = next(k for k in (5, 4, 3, 2, 1) if inner % k == 0)

        def rows(it, a):
            for k in range(group):
                i = 1 + it * group + k
                a = use(i, stencil(field, i, field[i - 1], field[i + 1], side), a)
            return a

        acc = lax.fori_loop(0, inner // group, rows, acc)
        end = LAT_DEV - 1
        return use(end, stencil(field, end, field[end - 1], down[...] * bottom_keep, side), acc)

    def keep_columns(i, row):
        rc_ref[0, pl.ds(i, 1), :] = row[0:1]
        rc_ref[1, pl.ds(i, 1), :] = row[LON_DEV - 1 : LON_DEV]

    zero = jnp.zeros((LON_DEV, LEV), F32)
    if mode == "first":

        def use(i, row, acc):
            r_out[i] = row
            keep_columns(i, row)
            return acc + row * row

    else:

        def use(i, row, acc):
            p = p_ref[i]
            q = p + row
            q_ref[i] = q
            return acc + p * q

    def scatter_sum():
        landed(parts)
        total = table_ref[me]
        for d in range(1, n):
            total = total + ta[d]
        bb[z] = total
        across = [send(bb.at[z], bb.at[z], b_s.at[d], b_r.at[d], to_lon(d)) for d in range(1, m)]
        pending.extend(across)
        return across

    def everywhere(buf, tile, ss, rs):
        buf[me] = tile
        copies = [send(buf.at[me], buf.at[me], ss.at[d], rs.at[d], to_lat(d)) for d in range(1, n)]
        pending.extend(copies)
        return copies

    def summed(buf, count):
        total = buf[0]
        for j in range(1, count):
            total = total + buf[j]
        return total

    def along_lon(buf, tile, ss, rs):
        buf[z] = tile
        copies = [send(buf.at[z], buf.at[z], ss.at[d], rs.at[d], to_lon(d)) for d in range(1, m)]
        pending.extend(copies)
        return copies

    if mode != "first":
        across = scatter_sum()
    landed(halos)
    ones = everywhere(s1, fold(sweep(g_ref, hu, hd, hc, use, zero)), s1_s, s1_r)
    if mode == "first":
        second = halo(r_out, rc_ref, hu2, hd2, hc2, k_s, k_r)
        across = scatter_sum()
    landed(across)
    gathers = everywhere(tf, summed(bb, m), c_s, c_r)
    landed(ones)
    crossing = along_lon(sc, summed(s1, n), sc_s, sc_r)
    landed(gathers)

    def tab(j):
        return tf[j // chunk, j % chunk]

    def spread(tile):
        return jnp.full((8, LANES), jnp.sum(tile), F32)

    rz_bias = jnp.zeros((8, LANES), F32)
    rr_bias = jnp.zeros((8, LANES), F32)
    if mode == "first":
        landed(owners)
        for j in range(width):
            rb = tab(j)
            bp = own_all[j // own, j % own]
            diag = bp + tab(width + j)
            pb = rb / diag
            rb_out[j], bp_out[j], diag_out[j], pb_out[j] = rb, bp, diag, pb
            rz_bias = rz_bias + rb * pb
            rr_bias = rr_bias + rb * rb
        rz_bias, rr_bias = spread(rz_bias), spread(rr_bias)
        landed(crossing)
        state_sum = spread(summed(sc, m))
        scal_out[...] = jnp.zeros(scal_out.shape, F32)
        scal_out[0] = state_sum + rz_bias
        scal_out[1] = state_sum + rr_bias
        landed(second)

        def use_u(i, row, acc):
            u_out[i] = row
            return acc

        sweep(r_out, hu2, hd2, hc2, use_u, 0)
    else:
        curve = jnp.zeros((8, LANES), F32)
        for j in range(width):
            pb = pb_ref[j]
            curve = curve + pb * (bp_ref[j] * pb + tab(j))
        curve = spread(curve)
        landed(crossing)
        alpha = scal_ref[0] / (spread(summed(sc, m)) + curve)
        line = alpha[0:1, :]

        def update(it, acc):
            for k in range(4):
                i = it * 4 + k
                row = r_ref[i] - line * q_ref[i]
                if mode == "middle":
                    r_out[i] = row
                    keep_columns(i, row)
                acc = acc + row * row
            return acc

        twos = everywhere(s2, fold(lax.fori_loop(0, LAT_DEV // 4, update, zero)), s2_s, s2_r)
        if mode == "middle":
            second = halo(r_out, rc_ref, hu2, hd2, hc2, k_s, k_r)
        for j in range(width):
            pb = pb_ref[j]
            rb = rb_ref[j] - alpha * (bp_ref[j] * pb + tab(j))
            zb = rb / diag_ref[j]
            if mode == "middle":
                rb_out[j] = rb
                x_out[j] = alpha * pb
            rz_bias = rz_bias + rb * zb
            rr_bias = rr_bias + rb * rb
        rz_bias, rr_bias = spread(rz_bias), spread(rr_bias)
        landed(twos)
        threes = along_lon(s3, summed(s2, n), s3_s, s3_r)
        if mode == "last":
            own = bias_out.shape[1] // LANES
            for j in range(own):
                bias_out[:, j * LANES : (j + 1) * LANES] = (
                    xb_ref[z * own + j] + alpha * pb_ref[z * own + j]
                )
        landed(threes)
        state_sum = spread(summed(s3, m))
        rz_new = state_sum + rz_bias
        scal_out[...] = scal_ref[...]
        scal_out[0] = rz_new
        scal_out[1 + turn] = state_sum + rr_bias
        scal_out[1 + ITERS + turn] = alpha
        if mode == "last":
            lane = lax.broadcasted_iota(jnp.int32, (8, LANES), 1)
            norms = jnp.zeros((8, LANES), F32)
            for j in range(ITERS + 1):
                norms = jnp.where(lane == j, scal_out[1 + j], norms)
            norms_out[...] = jnp.sqrt(norms)
        if mode == "middle":
            beta = rz_new / scal_ref[0]
            slope = beta[0:1, :]
            for j in range(width):
                pb_out[j] = rb_out[j] / diag_ref[j] + beta * pb_ref[j]
            landed(second)

            def use_u(i, row, acc):
                u_out[i] = row + slope * u_ref[i]
                p_out[i] = r_out[i] + slope * p_ref[i]
                return acc

            sweep(r_out, hu2, hd2, hc2, use_u, 0)
    for copy in pending:
        copy.wait_send()


VM = pl.BlockSpec(memory_space=pltpu.VMEM)
SM = pl.BlockSpec(memory_space=pltpu.SMEM)


def shaped(*shape):
    return jax.ShapeDtypeStruct(shape, F32)


def body(
    innovations,
    obs_precision,
    jacobian,
    predictors,
    obs_column,
    obs_channel,
    obs_count,
    smoothing,
    bias_precision,
):
    n = lax.axis_size("swath")
    m = lax.axis_size("chan")
    owned_width = bias_precision.shape[1]
    own = owned_width // LANES
    width = own * m
    blocks = owned_width * m // CH_BLOCK
    slots = obs_precision.shape[0]
    lines = slots // OBS_BLOCK
    grid_lines = lambda a: a.reshape(lines, OBS_BLOCK)
    cells = grid_lines(obs_column)
    line_rows = cells[:, 0] // LON_DEV
    common = (
        line_rows, obs_count, cells, grid_lines(obs_channel), grid_lines(obs_precision),
        predictors, jacobian,
    )
    field = shaped(LAT_DEV, LON_DEV, LEV)
    cols = shaped(2, LAT_DEV, LEV)
    tab = shaped(width, NPRED, LANES)
    scal = shaped(2 + 2 * ITERS, 8, LANES)
    smooth = smoothing.reshape(1, LEV)

    def local(init, *extra):
        used = (2 if init else 1) * width
        padded = -(-used // n) * n
        acc_rows = (2 if init else 1) * NPRED * blocks
        scratch = [pltpu.VMEM((acc_rows, CH_BLOCK), F32)]
        if not init:
            scratch += [
                pltpu.VMEM((LAT_DEV, LON_DEV, 2 * LEV), BF16),
                pltpu.VMEM((NPRED * blocks, CH_BLOCK), F32),
            ]
        out = pl.pallas_call(
            functools.partial(local_kernel, init, blocks),
            out_shape=(field, cols, shaped(padded, NPRED, LANES)),
            in_specs=[SM, SM] + [VM] * (len(common) - 2 + len(extra)),
            out_specs=(VM, VM, VM),
            scratch_shapes=scratch,
            compiler_params=pltpu.CompilerParams(vmem_limit_bytes=VMEM_LIMIT),
            name="local_first" if init else "local_next",
        )(*common, *extra)
        return out[0], out[1], out[2].reshape(n, padded // n, NPRED, LANES)

    def comm(mode, ident, outs, table, *args):
        chunk = table.shape[1]
        sem = lambda k: [pltpu.SemaphoreType.DMA((k,)), pltpu.SemaphoreType.DMA((k,))]
        vm = lambda *s: pltpu.VMEM(s, F32)
        scratch = [
            vm(n, chunk, NPRED, LANES), vm(n, chunk, NPRED, LANES), vm(m, chunk, NPRED, LANES),
            vm(n, 8, LANES), vm(m, 8, LANES), vm(LON_DEV, LEV), vm(LON_DEV, LEV), vm(2, LAT_DEV, LEV),
        ] + sem(n) + sem(4) + sem(n) + sem(m) + sem(n) + sem(m)
        if mode == "first":
            scratch += [vm(m, own, NPRED, LANES)] + sem(m)
        if mode != "first":
            scratch += [vm(LAT_DEV, LON_DEV, LEV), vm(n, 8, LANES), vm(m, 8, LANES)] + sem(n) + sem(m)
        if mode != "last":
            scratch += [vm(LON_DEV, LEV), vm(LON_DEV, LEV), vm(2, LAT_DEV, LEV)] + sem(4)
        return pl.pallas_call(
            functools.partial(comm_kernel, n, m, width, mode, ident),
            out_shape=outs,
            in_specs=[VM] * (4 + len(args)),
            out_specs=jax.tree.map(lambda _: VM, outs),
            scratch_shapes=scratch,
            compiler_params=pltpu.CompilerParams(
                collective_id=ident, has_side_effects=True, vmem_limit_bytes=VMEM_LIMIT
            ),
            name="comm_" + mode,
        )(smooth, *grads, table, *args)

    g, gc, table = local(True, grid_lines(innovations))
    grads = (g, gc)
    r, _, u, rb, diag, bp, pb, sc = comm(
        "first", 0, (field, cols, field, tab, tab, tab, tab, scal), table, bias_precision
    )
    p = r
    state = None
    total = None
    for turn in range(1, ITERS + 1):
        g, gc, table = local(False, u, pb)
        grads = (g, gc)
        args = (p, r, pb, rb, diag, bp, sc)
        old_p = p
        if turn < ITERS:
            outs = (field, cols, field, field, tab, tab, scal, tab)
            r, _, p, u, rb, pb, sc, total = comm("middle", turn, outs, table, *args, u)
        else:
            outs = (scal, shaped(8, LANES), shaped(NPRED, owned_width))
            sc, norms, bias = comm("last", turn, outs, table, *args, total)
        length = sc[1 + ITERS + turn, 0]
        state = length * old_p if state is None else state + length * old_p
    return (state, bias, norms[0, : ITERS + 1])


def solution(mesh):
    placed = (
        P(("swath", "chan")),
        P(("swath", "chan")),
        P(("swath", "chan"), None),
        P(None, ("swath", "chan")),
        P(("swath", "chan")),
        P(("swath", "chan")),
        P("swath", "chan"),
        P(),
        P(None, "chan"),
    )
    return jax.shard_map(
        body,
        mesh=mesh,
        in_specs=placed,
        out_specs=(P("swath", "chan", None), P(None, "chan"), P()),
        check_vma=False,
    )
```
